32 devices in a mesh: row: 4 (over z), col: 8 (over y, x, core).
Axes of the slice: x: 2, y: 2, z: 4, core: 2. Of those that a mesh axis runs over, the one named last changes fastest.
Arguments:
- q_halves: float32 [2, 5120, 5120], P(None, 'row', 'col'), may hold values from -6 to 6
- pole_values: float32 [10240], replicated, may hold values from -10240 to 10240, as said below
- weights: float32 [10240], replicated, may hold values from -6 to 6
- secular_roots: float32 [10240], replicated, may hold values from -10240 to 20480, as said below
- column_order: int32 [10240], replicated, may hold values from 0 to 10239, each once
- deflated: int32 [10240], replicated, may hold values 0 or 1
- reflectors: float32 [2, 2, 5120, 256], P(None, None, 'row'), may hold values from -0.0625 to 0.0625
- triangles: float32 [2, 256, 256], replicated, may hold values from -1.5 to 1.5
Outputs:
- eigvecs: float32 [2, 5120, 10240], P(None, 'row', 'col')
The draws below stay inside these ranges and needn't reach their ends.
Inputs may be any that keep to these rules, and one draw needn't show every extreme that they name: `pole_values`: all distinct; sorted, neighbouring poles differ by 0.5 to 1.5. The order of the entries is not sorted. secular_roots[j] lies above pole_values[j], at a quarter to three quarters of the distance to the next larger pole (for the largest pole, of a distance of 0.5 to 1.5), so every pole differs from every root by an eighth or more.
All inputs are finite; a program needn't handle non-finite values.
Results may differ from the reference program's by a relative error of at most 0.00015.
Values sent between devices are 32-bit elements; how exact they have to be, the bound alone decides.
No kernel may reach another device: no remote copies, remote signals or barrier semaphores. Data moves between devices by JAX's collectives and lax.ppermute only.
A program may use at most 192 MiB of HBM per device.

```python
import jax
import jax.numpy as jnp
from jax import lax

H = 5120
B = 256
N = 10240


def secular_pair(key):
    base = jax.random.fold_in(key, 4242)
    gaps = jax.random.uniform(jax.random.fold_in(base, 1), (N,), jnp.float32, 0.5, 1.5)
    fracs = jax.random.uniform(jax.random.fold_in(base, 2), (N,), jnp.float32, 0.25, 0.75)
    sorted_poles = jnp.cumsum(gaps) - 0.5 * N
    following = jnp.concatenate([gaps[1:], gaps[:1]])
    sorted_roots = sorted_poles + fracs * following
    shuffle = jax.random.permutation(jax.random.fold_in(base, 3), N)
    return (jnp.take(sorted_poles, shuffle), jnp.take(sorted_roots, shuffle))


def draw_pole_values(key, part):
    return secular_pair(key)[0]


def draw_secular_roots(key, part):
    return secular_pair(key)[1]


def set_ends(drawn, own_key, smallest, largest):
    shape = drawn.shape
    spot = [jax.random.randint(jax.random.fold_in(own_key, axis), (), 0, shape[axis]) for axis in range(len(shape))]
    drawn = drawn.at[tuple(spot)].set(smallest)
    longest = shape.index(max(shape))
    spot[longest] = (spot[longest] + 1) % shape[longest]
    return drawn.at[tuple(spot)].set(largest)


def shard_levels(key, shape, split, low, high):
    factor_of = 1.0
    for position, parts in split:
        draws = jax.random.uniform(jax.random.fold_in(jax.random.fold_in(key, 6), position), (parts,), jnp.float32, low / len(split), high / len(split))
        factor_of = factor_of * jnp.repeat(jnp.exp(draws), shape[position] // parts).reshape((-1,) + (1,) * (len(shape) - 1 - position))
    return factor_of


def bell_draw(rng, extent, width, most, cuts=(), held_as=jnp.bfloat16):
    result = jax.random.normal(rng, extent, jnp.float32) * width
    if len(cuts) > 0:
        result = shard_levels(rng, extent, cuts, -0.22, 0.18) * result
    return jnp.clip(result, min=-most, max=most).astype(held_as)


def setup_inputs(seed: int = 0) -> dict:
    arg_keys = jax.random.split(jax.random.key(seed), 9)
    return {
        "q_halves": bell_draw(arg_keys[0], (2, H, H), 1.0, 6.0, ((1, 4), (2, 8)), jnp.float32),
        "pole_values": draw_pole_values(jax.random.fold_in(arg_keys[8], 71), 0),
        "weights": bell_draw(arg_keys[2], (N,), 1.0, 6.0, (), jnp.float32),
        "secular_roots": draw_secular_roots(jax.random.fold_in(arg_keys[8], 71), 0),
        "column_order": jax.random.permutation(arg_keys[4], N).astype(jnp.int32),
        "deflated": set_ends((jax.random.randint(arg_keys[5], (N,), 0, 4) < 1).astype(jnp.int32), jax.random.fold_in(arg_keys[5], 1), 0, 1),
        "reflectors": bell_draw(arg_keys[6], (2, 2, H, B), N ** -0.5, 0.0625, ((2, 4),), jnp.float32),
        "triangles": bell_draw(arg_keys[7], (2, B, B), 0.25, 1.5, (), jnp.float32),
    }


EPSILON = 1e-06

def column_scale(zeds, pole_values, chosen_roots):
    ratio = zeds[:, None] / (pole_values[:, None] - chosen_roots[None, :])
    return lax.rsqrt(lax.optimization_barrier(jnp.sum(ratio * ratio, axis=0)) + EPSILON)

def cauchy_tile(zeds, pole_values, secular_roots, deflated, first_row, row_count, source, scale):
    pole_slice = lax.dynamic_slice_in_dim(pole_values, first_row, row_count)
    zed_slice = lax.dynamic_slice_in_dim(zeds, first_row, row_count)
    chosen = jnp.take(secular_roots, source)
    cauchy = zed_slice[:, None] / (pole_slice[:, None] - chosen[None, :]) * scale[None, :]
    row_ids = first_row + jnp.arange(row_count, dtype=jnp.int32)
    unit = (row_ids[:, None] == source[None, :]).astype(cauchy.dtype)
    return jnp.where(jnp.take(deflated, source)[None, :] > 0, unit, cauchy)

def project(vectors, field):
    return jnp.einsum('hrb,hrc->bc', vectors, field, precision=lax.Precision.HIGHEST)

def expand(vectors, coef):
    return jnp.einsum('hrb,bc->hrc', vectors, coef, precision=lax.Precision.HIGHEST)

def reference(q_halves, pole_values, weights, secular_roots, column_order, deflated, reflectors, triangles):
    half = q_halves.shape[1]
    zeds = weights * (1 - deflated).astype(weights.dtype)
    scale = column_scale(zeds, pole_values, jnp.take(secular_roots, column_order))
    mixed = jnp.stack([jnp.dot(q_halves[which], cauchy_tile(zeds, pole_values, secular_roots, deflated, which * half, half, column_order, scale), precision=lax.Precision.HIGHEST) for which in range(2)])
    upper = jnp.triu(triangles)
    second = mixed - expand(reflectors[1], jnp.dot(upper[1], project(reflectors[1], mixed), precision=lax.Precision.HIGHEST))
    return second - expand(reflectors[0], jnp.dot(upper[0], project(reflectors[0], second), precision=lax.Precision.HIGHEST))
```

```python
import functools

import jax
import jax.numpy as jnp
from jax import lax
from jax.experimental import pallas as pl
from jax.experimental.pallas import tpu as pltpu
from jax.sharding import PartitionSpec as P

EPSILON = 1e-06
FAR = 3e38


def split2(x):
    high = x.astype(jnp.bfloat16)
    return high, (x - high.astype(jnp.float32)).astype(jnp.bfloat16)


def dot3(a_high, a_low, b_high, b_low):
    dot = functools.partial(jnp.dot, preferred_element_type=jnp.float32)
    return dot(a_high, b_high) + (dot(a_high, b_low) + dot(a_low, b_high))


def cauchy_kernel(pole_ref, zed_ref, root_ref, key_ref, high_ref, low_ref, total_ref):
    step = pl.program_id(0)
    rows = pole_ref.shape[0]

    @pl.when(step == 0)
    def _():
        total_ref[...] = jnp.zeros_like(total_ref)

    ratio = zed_ref[...] / (pole_ref[...] - root_ref[...])
    total_ref[...] += jnp.sum(ratio * ratio, axis=0, keepdims=True)
    row_ids = step * rows + lax.broadcasted_iota(jnp.int32, ratio.shape, 0)
    value = jnp.where(row_ids == key_ref[...], 1.0, ratio)
    high_ref[...], low_ref[...] = split2(value)


def make_cauchy(poles, zeds, roots, keys):
    count, width = poles.shape[0], roots.shape[0]
    rows = 256
    vec = pl.BlockSpec((rows, 1), lambda i: (i, 0))
    line = pl.BlockSpec((1, width), lambda i: (0, 0))
    tile = pl.BlockSpec((rows, width), lambda i: (i, 0))
    part = jax.ShapeDtypeStruct((count, width), jnp.bfloat16)
    return pl.pallas_call(
        cauchy_kernel,
        grid=(count // rows,),
        in_specs=[vec, vec, line, line],
        out_specs=[tile, tile, line],
        out_shape=[part, part, jax.ShapeDtypeStruct((1, width), jnp.float32)],
        name="cauchy",
    )(poles[:, None], zeds[:, None], roots[None, :], keys[None, :])


def early_kernel(r_ref, ch_ref, cl_ref, o_ref, high, low):
    @pl.when(pl.program_id(0) == 0)
    def _():
        for h in range(2):
            half = r_ref.shape[2]
            high[:, h * half : (h + 1) * half], low[:, h * half : (h + 1) * half] = split2(r_ref[h])

    o_ref[...] = dot3(high[...], low[...], ch_ref[...], cl_ref[...])


def early_projection(r_all, c_high, c_low):
    _, rows, half = r_all.shape
    count, width = c_high.shape
    tile = 128
    col = pl.BlockSpec((count, tile), lambda j: (0, j))
    return pl.pallas_call(
        early_kernel,
        grid=(width // tile,),
        in_specs=[pl.BlockSpec(r_all.shape, lambda j: (0, 0, 0)), col, col],
        out_specs=pl.BlockSpec((rows, tile), lambda j: (0, j)),
        out_shape=jax.ShapeDtypeStruct((rows, width), jnp.float32),
        scratch_shapes=[pltpu.VMEM((rows, count), jnp.bfloat16)] * 2,
        name="early",
    )(r_all, c_high, c_low)


def rows_kernel(pairs, last, info_ref, *refs):
    refs = list(refs)
    pieces = [refs.pop(0) for _ in range(2 * pairs)]
    highs = [refs.pop(0) for _ in range(pairs)]
    lows = [refs.pop(0) for _ in range(pairs)]
    if last:
        first_y, second_y, s_ref, scale_ref = (refs.pop(0) for _ in range(4))
    acc_ref = refs.pop(0)
    out_ref, q_high, q_low = refs[:3]
    depth = pieces[0].shape[2]
    odd = info_ref[0] > 0

    @pl.when(pl.program_id(1) == 0)
    def _():
        for i in range(pairs):
            mine, other = pieces[2 * i][0], pieces[2 * i + 1][0]
            ordered = (jnp.where(odd, other, mine), jnp.where(odd, mine, other))
            for core in range(2):
                span = slice(core * depth, (core + 1) * depth)
                q_high[i, :, span], q_low[i, :, span] = split2(ordered[core])
        if last:
            block = first_y.shape[3]
            y_high, y_low = refs[3:]
            y_high[:, :block], y_low[:, :block] = split2(first_y[0, 0])
            y_high[:, block:], y_low[:, block:] = split2(second_y[0, 0])

    total = sum(dot3(q_high[i], q_low[i], highs[i][...], lows[i][...]) for i in range(pairs))
    if last:
        y_high, y_low = refs[3:]
        total = total + acc_ref[0] - dot3(y_high[...], y_low[...], *split2(s_ref[...]))
        total = total * scale_ref[...]
    out_ref[0] = total


def rows_call(info, pieces, row_blocks, c_high, c_low, held, held_shape, block, rows, finish=None):
    pairs = len(pieces) // 2
    depth = pieces[0].shape[2]
    width = c_high.shape[1]
    tile = 256 if width % 256 == 0 else 128

    def piece_spec(at):
        return pl.BlockSpec((1, rows, depth), lambda h, j, info: (h, at, 0))

    def cauchy_spec(i):
        return pl.BlockSpec((2 * depth, tile), lambda h, j, info: (h * info[1] + info[2 + i], j))

    in_specs = [piece_spec(at) for at in row_blocks]
    in_specs += [cauchy_spec(i) for i in range(pairs)] * 2
    operands = list(pieces) + [c_high] * pairs + [c_low] * pairs
    out_spec = pl.BlockSpec((1, rows, tile), lambda h, j, info: (h, block, j))
    scratch = [pltpu.VMEM((pairs, rows, 2 * depth), jnp.bfloat16)] * 2
    if finish is not None:
        reflectors, s, scale = finish
        size = reflectors.shape[3]
        in_specs += [
            pl.BlockSpec((1, 1, rows, size), lambda h, j, info: (0, h, block, 0)),
            pl.BlockSpec((1, 1, rows, size), lambda h, j, info: (1, h, block, 0)),
            pl.BlockSpec((2 * size, tile), lambda h, j, info: (0, j)),
            pl.BlockSpec((1, tile), lambda h, j, info: (0, j)),
        ]
        operands += [reflectors, reflectors, s, scale]
        scratch += [pltpu.VMEM((rows, 2 * size), jnp.bfloat16)] * 2
        in_specs.append(out_spec)
    else:
        in_specs.append(pl.BlockSpec(memory_space=pl.ANY))
    aliases = {1 + len(operands): 0}
    operands.append(held)
    return pl.pallas_call(
        functools.partial(rows_kernel, pairs, finish is not None),
        grid_spec=pltpu.PrefetchScalarGridSpec(
            num_scalar_prefetch=1,
            grid=(2, width // tile),
            in_specs=in_specs,
            out_specs=out_spec,
            scratch_shapes=scratch,
        ),
        out_shape=jax.ShapeDtypeStruct(held_shape, jnp.float32),
        input_output_aliases=aliases,
        name="finish" if finish is not None else "rows",
    )(info, *operands)


def local(
    q_halves, pole_values, weights, secular_roots, column_order, deflated, reflectors, triangles
):
    col_count = lax.axis_size("col")
    me = lax.axis_index("col")
    _, rows, depth = q_halves.shape
    width = 2 * depth
    exact = dict(precision=lax.Precision.HIGHEST)

    def swap(x, mask):
        return lax.ppermute(x, "col", [(i, i ^ mask) for i in range(col_count)])

    unit = rows // 10
    sizes = [2 * unit] * 4 + [unit] * 2
    starts = [sum(sizes[:i]) for i in range(len(sizes))]
    bits = [1 << b for b in range(1, (col_count - 1).bit_length())]
    partner = swap(q_halves, 1)
    own = [lax.slice_in_dim(q_halves, a, a + n, axis=1) for a, n in zip(starts, sizes)]
    got = [{} for _ in sizes]
    for c in range(len(sizes)):
        for bit in bits:
            got[c][bit] = swap(own[c], bit)

    stacked = jnp.concatenate([reflectors[0], reflectors[1]], axis=2)
    r_part = jnp.einsum("hrb,hrk->hbk", stacked, q_halves, **exact)
    r_part = lax.psum_scatter(r_part, "row", scatter_dimension=1, tiled=True)
    r_all = lax.all_gather(r_part, "col", axis=2, tiled=True)
    cross = lax.psum(jnp.einsum("hrb,hrd->bd", reflectors[0], reflectors[1], **exact), "row")

    zeds = weights * (1 - deflated).astype(jnp.float32)
    source = lax.dynamic_slice_in_dim(column_order, me * width, width)
    roots = jnp.take(jnp.where(deflated > 0, FAR, secular_roots), source)
    gone = roots > 1e38
    keys = jnp.where(gone, source, -1)
    c_high, c_low, total = make_cauchy(pole_values, zeds, roots, keys)
    scale = jnp.where(gone[None, :], 1.0, lax.rsqrt(total + EPSILON))

    for c in range(len(sizes)):
        for mask in range(2, col_count, 2):
            if mask not in got[c]:
                set_bits = [b for b in bits if b & mask]
                bit = set_bits[0] if c % 2 == 0 else set_bits[-1]
                got[c][mask] = swap(got[c][mask ^ bit], bit)
        for mask in range(2, col_count, 2):
            got[c][mask + 1] = swap(got[c][mask], 1)

    def info_for(masks):
        head = [me & 1, jnp.int32(col_count // 2)]
        return jnp.stack(head + [(me ^ m) >> 1 for m in masks]).astype(jnp.int32)

    near = [0] + bits
    far = [m for m in range(2, col_count, 2) if m not in bits]
    out_shape = (2, rows, width)
    held = jnp.zeros(out_shape, jnp.float32)
    for c, n in enumerate(sizes):
        block = starts[c] // n
        pieces, blocks = [], []
        for m in near:
            pieces += [q_halves, partner] if m == 0 else [got[c][m], got[c][m + 1]]
            blocks += [block, block] if m == 0 else [0, 0]
        held = rows_call(info_for(near), pieces, blocks, c_high, c_low, held, out_shape, block, n)

    p_part = early_projection(r_all, c_high, c_low)
    p_all = lax.all_gather(p_part, "row", axis=0, tiled=True)
    size = triangles.shape[1]
    upper = jnp.triu(triangles)
    s1 = jnp.dot(upper[1], p_all[size:], **exact)
    s0 = jnp.dot(upper[0], p_all[:size] - jnp.dot(cross, s1, **exact), **exact)
    finish = (reflectors, jnp.concatenate([s0, s1], axis=0), scale)

    for c, n in enumerate(sizes):
        block = starts[c] // n
        pieces = [got[c][m + k] for m in far for k in range(2)]
        blocks = [0] * len(pieces)
        held = rows_call(
            info_for(far), pieces, blocks, c_high, c_low, held, out_shape, block, n, finish
        )
    return held


def solution(mesh):
    placed = (P(None, "row", "col"), P(), P(), P(), P(), P(), P(None, None, "row", None), P())
    return jax.shard_map(
        local, mesh=mesh, in_specs=placed, out_specs=P(None, "row", "col"), check_vma=False
    )
```

```python
import functools

import jax
import jax.numpy as jnp
from jax import lax
from jax.experimental import pallas as pl
from jax.experimental.pallas import tpu as pltpu
from jax.sharding import PartitionSpec as P


EPSILON = 1e-06
FAR = 3e38


def split2(x):
    high = x.astype(jnp.bfloat16)
    return high, (x - high.astype(jnp.float32)).astype(jnp.bfloat16)


def dot3(a_high, a_low, b_high, b_low):
    dot = functools.partial(jnp.dot, preferred_element_type=jnp.float32)
    return dot(a_high, b_high) + (dot(a_high, b_low) + dot(a_low, b_high))


def cauchy_kernel(pole_ref, zed_ref, root_ref, key_ref, high_ref, low_ref, total_ref):
    step = pl.program_id(0)
    rows = pole_ref.shape[0]

    @pl.when(step == 0)
    def _():
        total_ref[...] = jnp.zeros_like(total_ref)

    ratio = zed_ref[...] / (pole_ref[...] - root_ref[...])
    total_ref[...] += jnp.sum(ratio * ratio, axis=0, keepdims=True)
    row_ids = step * rows + lax.broadcasted_iota(jnp.int32, ratio.shape, 0)
    value = jnp.where(row_ids == key_ref[...], 1.0, ratio)
    high_ref[...], low_ref[...] = split2(value)


def make_cauchy(poles, zeds, roots, keys):
    count, width = poles.shape[0], roots.shape[0]
    rows = 256
    vec = pl.BlockSpec((rows, 1), lambda i: (i, 0))
    line = pl.BlockSpec((1, width), lambda i: (0, 0))
    tile = pl.BlockSpec((rows, width), lambda i: (i, 0))
    part = jax.ShapeDtypeStruct((count, width), jnp.bfloat16)
    return pl.pallas_call(
        cauchy_kernel,
        grid=(count // rows,),
        in_specs=[vec, vec, line, line],
        out_specs=[tile, tile, line],
        out_shape=[part, part, jax.ShapeDtypeStruct((1, width), jnp.float32)],
        name="cauchy",
    )(poles[:, None], zeds[:, None], roots[None, :], keys[None, :])


def early_kernel(r_ref, ch_ref, cl_ref, o_ref, high, low):
    @pl.when(pl.program_id(0) == 0)
    def _():
        for h in range(2):
            half = r_ref.shape[2]
            high[:, h * half : (h + 1) * half], low[:, h * half : (h + 1) * half] = split2(r_ref[h])

    o_ref[...] = dot3(high[...], low[...], ch_ref[...], cl_ref[...])


def early_projection(r_all, c_high, c_low):
    _, rows, _ = r_all.shape
    count, width = c_high.shape
    tile = 128
    col = pl.BlockSpec((count, tile), lambda j: (0, j))
    return pl.pallas_call(
        early_kernel,
        grid=(width // tile,),
        in_specs=[pl.BlockSpec(r_all.shape, lambda j: (0, 0, 0)), col, col],
        out_specs=pl.BlockSpec((rows, tile), lambda j: (0, j)),
        out_shape=jax.ShapeDtypeStruct((rows, width), jnp.float32),
        scratch_shapes=[pltpu.VMEM((rows, count), jnp.bfloat16)] * 2,
        name="early",
    )(r_all, c_high, c_low)


def rows_kernel(counts, last, info_ref, *refs):
    refs = list(refs)
    pairs, parts, rows = counts
    sources = [[[refs.pop(0) for _ in range(parts)] for _ in range(2)] for _ in range(pairs)]
    high_ref, low_ref = refs.pop(0), refs.pop(0)
    if last:
        first_y, second_y, s_ref, scale_ref, acc_ref = (refs.pop(0) for _ in range(5))
    refs = refs[1:] if last == 2 else refs
    out_ref, staged, q_high, q_low, sems = refs[:5]
    depth = staged.shape[3]
    step, col = pl.program_id(0), pl.program_id(1)
    half, block, odd = info_ref[0], info_ref[1], info_ref[2]

    def copies(i):
        for core in range(2):
            slot = odd if core == 0 else 1 - odd
            for part in range(parts):
                ref = sources[i][core][part]
                if len(ref.shape) == 3:
                    ref = ref.at[half, pl.ds((block * parts + part) * rows, rows)]
                yield pltpu.make_async_copy(
                    ref, staged.at[slot, part], sems.at[core, part]
                )

    @pl.when(jnp.logical_and(step == 0, col == 0))
    def _():
        for copy in copies(0):
            copy.start()

    for i in range(pairs):

        @pl.when(jnp.logical_and(step == i, col == 0))
        def _():
            for copy in copies(i):
                copy.wait()
            for core in range(2):
                for part in range(parts):
                    at = (slice(part * rows, (part + 1) * rows), slice(core * depth, (core + 1) * depth))
                    q_high[at], q_low[at] = split2(staged[core, part])
            if i + 1 < pairs:
                for copy in copies(i + 1):
                    copy.start()

    product = dot3(q_high[...], q_low[...], high_ref[...], low_ref[...])

    def emit(mixed):
        if not last:
            out_ref[...] = mixed
            return
        size = first_y.shape[3]
        y_high, y_low = refs[5:7]

        @pl.when(col == 0)
        def _():
            y_high[:, :size], y_low[:, :size] = split2(first_y[0, 0])
            y_high[:, size:], y_low[:, size:] = split2(second_y[0, 0])

        update = dot3(y_high[...], y_low[...], *split2(s_ref[...]))
        out_ref[0] = (acc_ref[...] + mixed - update) * scale_ref[...]

    if pairs == 1:
        emit(product)
    else:
        total = refs[-1]

        @pl.when(step == 0)
        def _():
            total[col] = product

        if pairs > 2:

            @pl.when(jnp.logical_and(step > 0, step < pairs - 1))
            def _():
                total[col] += product

        @pl.when(step == pairs - 1)
        def _():
            emit(total[col] + product)


def rows_call(half, block, masks, pieces, c_high, c_low, finish=None):
    me = lax.axis_index("col")
    chips = lax.axis_size("col") // 2
    pairs, parts = len(masks), len(pieces[0][0])
    rows, depth = pieces[-1][0][0].shape[-2:]
    width = c_high.shape[1]
    tile = 256 if width % 256 == 0 else 128
    head = [jnp.int32(half), jnp.int32(block), me & 1]
    info = jnp.stack(head + [half * chips + ((me ^ m) >> 1) for m in masks]).astype(jnp.int32)

    operands = [array for pair in pieces for piece in pair for array in piece]
    in_specs = [pl.BlockSpec(memory_space=pl.ANY)] * len(operands)
    cauchy = pl.BlockSpec((2 * depth, tile), lambda i, j, info: (info[3 + i], j))
    in_specs += [cauchy, cauchy]
    operands += [c_high, c_low]
    count = parts * rows
    scratch = [pltpu.VMEM((2, parts, rows, depth), jnp.float32)]
    scratch += [pltpu.VMEM((count, 2 * depth), jnp.bfloat16)] * 2
    scratch += [pltpu.SemaphoreType.DMA((2, parts))]
    aliases, last = {}, 0
    if finish is None:
        out_shape = (count, width)
        out_spec = pl.BlockSpec((count, tile), lambda i, j, info: (0, jnp.where(i == pairs - 1, j, 0)))
    else:
        reflectors, s, scale, held, out = finish
        last = 1 if out is None else 2
        size = reflectors.shape[3]
        in_specs += [
            pl.BlockSpec((1, 1, count, size), lambda i, j, info: (0, half, block, 0)),
            pl.BlockSpec((1, 1, count, size), lambda i, j, info: (1, half, block, 0)),
            pl.BlockSpec((2 * size, tile), lambda i, j, info: (0, j)),
            pl.BlockSpec((1, tile), lambda i, j, info: (0, j)),
            pl.BlockSpec((count, tile), lambda i, j, info: (block, j)),
        ]
        operands += [reflectors, reflectors, s, scale, held]
        if out is not None:
            in_specs.append(pl.BlockSpec(memory_space=pl.ANY))
            operands.append(out)
            aliases = {len(operands): 0}
        out_shape = (2, held.shape[0], width)
        out_spec = pl.BlockSpec(
            (1, count, tile), lambda i, j, info: (half, block, jnp.where(i == pairs - 1, j, 0))
        )
        scratch += [pltpu.VMEM((count, 2 * size), jnp.bfloat16)] * 2
    if pairs > 1:
        scratch.append(pltpu.VMEM((width // tile, count, tile), jnp.float32))
    return pl.pallas_call(
        functools.partial(rows_kernel, (pairs, parts, rows), last),
        grid_spec=pltpu.PrefetchScalarGridSpec(
            num_scalar_prefetch=1,
            grid=(pairs, width // tile),
            in_specs=in_specs,
            out_specs=out_spec,
            scratch_shapes=scratch,
        ),
        out_shape=jax.ShapeDtypeStruct(out_shape, jnp.float32),
        input_output_aliases=aliases,
    )(info, *operands)


def project_kernel(y_ref, q_ref, o_ref, q_high, q_low):
    @pl.when(pl.program_id(1) == 0)
    def _():
        q_high[...], q_low[...] = split2(q_ref[0])

    o_ref[0] = dot3(*split2(y_ref[0, 0].T), q_high[...], q_low[...])


def project(reflectors, q_halves):
    _, rows, depth = q_halves.shape
    size = reflectors.shape[3]
    return pl.pallas_call(
        project_kernel,
        grid=(2, 2),
        in_specs=[
            pl.BlockSpec((1, 1, rows, size), lambda h, i: (i, h, 0, 0)),
            pl.BlockSpec((1, rows, depth), lambda h, i: (h, 0, 0)),
        ],
        out_specs=pl.BlockSpec((1, size, depth), lambda h, i: (h, i, 0)),
        out_shape=jax.ShapeDtypeStruct((2, 2 * size, depth), jnp.float32),
        scratch_shapes=[pltpu.VMEM((rows, depth), jnp.bfloat16)] * 2,
        name="project",
    )(reflectors, q_halves)


def merge(
    q_halves, pole_values, weights, secular_roots, column_order, deflated, reflectors, triangles
):
    col_count, row_count = lax.axis_size("col"), lax.axis_size("row")
    me, my_row = lax.axis_index("col"), lax.axis_index("row")
    _, rows, depth = q_halves.shape
    width = 2 * depth
    exact = dict(precision=lax.Precision.HIGHEST)
    cut = rows // 2

    def swap(x, mask):
        return lax.ppermute(x, "col", [(i, i ^ mask) for i in range(col_count)])

    def row_swap(x, mask):
        return lax.ppermute(x, "row", [(i, i ^ mask) for i in range(row_count)])

    bits = [1 << b for b in range(1, (col_count - 1).bit_length())]
    near = [0] + bits
    far = [m for m in range(2, col_count, 2) if m not in bits]

    partner = swap(q_halves, 1)
    got = [{} for _ in range(2)]
    for h in range(2):
        own = [q_halves[h, :cut], q_halves[h, cut:]]
        for bit in bits:
            order = (1, 0) if bit == bits[0] else (0, 1)
            parts = {p: swap(own[p], bit) for p in order}
            got[h][bit] = [parts[0], parts[1]]
    for h in range(2):
        for m in far:
            set_bits = [b for b in bits if b & m]
            via = [set_bits[0], set_bits[-1]]
            got[h][m] = [swap(got[h][m ^ via[p]][p], via[p]) for p in range(2)]
        for m in bits + far:
            got[h][m + 1] = [swap(x, 1) for x in got[h][m]]

    r_part = project(reflectors, q_halves)
    share = r_part.shape[1] // row_count
    r_mine = lax.dynamic_slice_in_dim(r_part, my_row * share, share, axis=1)
    for m in range(1, row_count):
        away = lax.dynamic_slice_in_dim(r_part, (my_row ^ m) * share, share, axis=1)
        r_mine = r_mine + row_swap(away, m)
    r_all = lax.all_gather(r_mine, "col", axis=2, tiled=True)
    cross = lax.psum(jnp.einsum("hrb,hrd->bd", reflectors[0], reflectors[1], **exact), "row")

    zeds = weights * (1 - deflated).astype(jnp.float32)
    source = lax.dynamic_slice_in_dim(column_order, me * width, width)
    roots = jnp.take(jnp.where(deflated > 0, FAR, secular_roots), source)
    gone = roots > 1e38
    keys = jnp.where(gone, source, -1)
    c_high, c_low, total = make_cauchy(pole_values, zeds, roots, keys)
    scale = jnp.where(gone[None, :], 1.0, lax.rsqrt(total + EPSILON))

    def pieces_of(h, masks, parts):
        pieces = []
        for m in masks:
            if m == 0:
                pieces.append([[q_halves] * len(parts), [partner] * len(parts)])
            else:
                pieces.append([[got[h][m + k][p] for p in parts] for k in range(2)])
        return pieces

    held = []
    for h in range(2):
        held.append(rows_call(h, 0, near, pieces_of(h, near, (0, 1)), c_high, c_low))

    p_part = early_projection(r_all, c_high, c_low)
    p_stack = jnp.stack([p_part] + [row_swap(p_part, m) for m in range(1, row_count)])
    p_all = jnp.concatenate(
        [lax.dynamic_index_in_dim(p_stack, my_row ^ z, keepdims=False) for z in range(row_count)]
    )
    size = triangles.shape[1]
    upper = jnp.triu(triangles)
    s1 = jnp.dot(upper[1], p_all[size:], **exact)
    s0 = jnp.dot(upper[0], p_all[:size] - jnp.dot(cross, s1, **exact), **exact)
    s = jnp.concatenate([s0, s1], axis=0)

    out = None
    for h in range(2):
        for block, parts in [(0, (0, 1))] if h == 0 else [(0, (0,)), (1, (1,))]:
            out = rows_call(
                h, block, far, pieces_of(h, far, parts), c_high, c_low,
                (reflectors, s, scale, held[h], out),
            )
    return out


def solution(mesh):
    placed = (P(None, "row", "col"), P(), P(), P(), P(), P(), P(None, None, "row", None), P())
    return jax.shard_map(
        merge, mesh=mesh, in_specs=placed, out_specs=P(None, "row", "col"), check_vma=False
    )
```

```python
import functools

import jax
import jax.numpy as jnp
from jax import lax
from jax.experimental import pallas as pl
from jax.experimental.pallas import tpu as pltpu
from jax.sharding import PartitionSpec as P


EPSILON = 1e-06
FAR = 3e38


def split2(x):
    high = x.astype(jnp.bfloat16)
    return high, (x - high.astype(jnp.float32)).astype(jnp.bfloat16)


def dot3(a_high, a_low, b_high, b_low):
    dot = functools.partial(jnp.dot, preferred_element_type=jnp.float32)
    return dot(a_high, b_high) + (dot(a_high, b_low) + dot(a_low, b_high))


def cauchy_kernel(pole_ref, zed_ref, root_ref, key_ref, high_ref, low_ref, total_ref, poles, zeds):
    step = pl.program_id(0)
    rows = high_ref.shape[0]
    chunk = 256

    @pl.when(step == 0)
    def _():
        total_ref[...] = jnp.zeros_like(total_ref)

    for ref, held in ((pole_ref, poles), (zed_ref, zeds)):
        held[...] = jnp.broadcast_to(ref[...], (8, rows)).T

    @pl.loop(0, rows // chunk)
    def _(i):
        at = pl.multiple_of(i * chunk, chunk)
        span = pl.ds(at, chunk)
        ratio = zeds[span, :1] / (poles[span, :1] - root_ref[...])
        total_ref[...] += jnp.sum(ratio * ratio, axis=0, keepdims=True)
        row_ids = step * rows + at + lax.broadcasted_iota(jnp.int32, ratio.shape, 0)
        value = jnp.where(row_ids == key_ref[...], 1.0, ratio)
        high_ref[span], low_ref[span] = split2(value)


def make_cauchy(poles, zeds, roots, keys):
    count, width = poles.shape[0], roots.shape[0]
    rows = count // 8
    vec = pl.BlockSpec((1, rows), lambda i: (0, i))
    line = pl.BlockSpec((1, width), lambda i: (0, 0))
    tile = pl.BlockSpec((rows, width), lambda i: (i, 0))
    part = jax.ShapeDtypeStruct((count, width), jnp.bfloat16)
    return pl.pallas_call(
        cauchy_kernel,
        grid=(count // rows,),
        in_specs=[vec, vec, line, line],
        out_specs=[tile, tile, line],
        out_shape=[part, part, jax.ShapeDtypeStruct((1, width), jnp.float32)],
        scratch_shapes=[pltpu.VMEM((rows, 8), jnp.float32)] * 2,
        name="cauchy",
    )(poles[None, :], zeds[None, :], roots[None, :], keys[None, :])


def early_kernel(r_ref, ch_ref, cl_ref, o_ref, high, low):
    @pl.when(pl.program_id(0) == 0)
    def _():
        for h in range(2):
            half = r_ref.shape[2]
            high[:, h * half : (h + 1) * half], low[:, h * half : (h + 1) * half] = split2(r_ref[h])

    o_ref[...] = dot3(high[...], low[...], ch_ref[...], cl_ref[...])


def early_projection(r_all, c_high, c_low):
    _, rows, _ = r_all.shape
    count, width = c_high.shape
    tile = 256 if width % 256 == 0 else 128
    col = pl.BlockSpec((count, tile), lambda j: (0, j))
    return pl.pallas_call(
        early_kernel,
        grid=(width // tile,),
        in_specs=[pl.BlockSpec(r_all.shape, lambda j: (0, 0, 0)), col, col],
        out_specs=pl.BlockSpec((rows, tile), lambda j: (0, j)),
        out_shape=jax.ShapeDtypeStruct((rows, width), jnp.float32),
        scratch_shapes=[pltpu.VMEM((rows, count), jnp.bfloat16)] * 2,
        name="early",
    )(r_all, c_high, c_low)


def rows_kernel(counts, last, info_ref, *refs):
    refs = list(refs)
    pairs, parts, rows = counts
    sources = [[[refs.pop(0) for _ in range(parts)] for _ in range(2)] for _ in range(pairs)]
    high_ref, low_ref = refs.pop(0), refs.pop(0)
    if last:
        first_y, second_y, sh_ref, sl_ref, scale_ref, acc_ref = (refs.pop(0) for _ in range(6))
    refs = refs[1:] if last == 2 else refs
    out_ref, staged, q_high, q_low, sems = refs[:5]
    depth = staged.shape[3]
    step, col = pl.program_id(0), pl.program_id(1)
    half, block, odd = info_ref[0], info_ref[1], info_ref[2]

    def copies(i):
        for core in range(2):
            slot = odd if core == 0 else 1 - odd
            for part in range(parts):
                ref = sources[i][core][part]
                if len(ref.shape) == 3:
                    ref = ref.at[half, pl.ds((block * parts + part) * rows, rows)]
                yield pltpu.make_async_copy(
                    ref, staged.at[slot, part], sems.at[core, part]
                )

    @pl.when(jnp.logical_and(step == 0, col == 0))
    def _():
        for copy in copies(0):
            copy.start()

    for i in range(pairs):

        @pl.when(jnp.logical_and(step == i, col == 0))
        def _():
            for copy in copies(i):
                copy.wait()
            for core in range(2):
                for part in range(parts):
                    at = (slice(part * rows, (part + 1) * rows), slice(core * depth, (core + 1) * depth))
                    q_high[at], q_low[at] = split2(staged[core, part])
            if i + 1 < pairs:
                for copy in copies(i + 1):
                    copy.start()

    def emit(mixed):
        if last:
            out_ref[0] = (acc_ref[...] + mixed) * scale_ref[...]
        else:
            out_ref[...] = mixed

    if last:
        size = first_y.shape[3]

        @pl.when(jnp.logical_and(step == 0, col == 0))
        def _():
            for at, y_ref in ((2 * depth, first_y), (2 * depth + size, second_y)):
                span = slice(at, at + size)
                q_high[:, span], q_low[:, span] = split2(y_ref[0, 0])

    high, low = high_ref[...], low_ref[...]
    if last:
        keep = jnp.where(step == 0, 1.0, 0.0).astype(jnp.bfloat16) if pairs > 1 else None
        extra = [ref[...] if keep is None else ref[...] * keep for ref in (sh_ref, sl_ref)]
        high, low = jnp.concatenate([high, extra[0]]), jnp.concatenate([low, extra[1]])
    product = dot3(q_high[...], q_low[...], high, low)

    if pairs == 1:
        emit(product)
    else:
        total = refs[-1]

        @pl.when(step == 0)
        def _():
            total[col] = product

        if pairs > 2:

            @pl.when(jnp.logical_and(step > 0, step < pairs - 1))
            def _():
                total[col] += product

        @pl.when(step == pairs - 1)
        def _():
            emit(total[col] + product)


def rows_call(half, block, masks, pieces, c_high, c_low, finish=None):
    me = lax.axis_index("col")
    chips = lax.axis_size("col") // 2
    pairs, parts = len(masks), len(pieces[0][0])
    rows, depth = pieces[-1][0][0].shape[-2:]
    width = c_high.shape[1]
    tile = 256 if width % 256 == 0 else 128
    head = [jnp.int32(half), jnp.int32(block), me & 1]
    info = jnp.stack(head + [half * chips + ((me ^ m) >> 1) for m in masks]).astype(jnp.int32)

    operands = [array for pair in pieces for piece in pair for array in piece]
    in_specs = [pl.BlockSpec(memory_space=pl.ANY)] * len(operands)
    cauchy = pl.BlockSpec((2 * depth, tile), lambda i, j, info: (info[3 + i], j))
    in_specs += [cauchy, cauchy]
    operands += [c_high, c_low]
    count = parts * rows
    scratch = [pltpu.VMEM((2, parts, rows, depth), jnp.float32)]
    inner = 2 * depth + (0 if finish is None else 2 * finish[0].shape[3])
    scratch += [pltpu.VMEM((count, inner), jnp.bfloat16)] * 2
    scratch += [pltpu.SemaphoreType.DMA((2, parts))]
    aliases, last = {}, 0
    if finish is None:
        out_shape = (count, width)
        out_spec = pl.BlockSpec((count, tile), lambda i, j, info: (0, jnp.where(i == pairs - 1, j, 0)))
    else:
        reflectors, s, scale, held, out = finish
        last = 1 if out is None else 2
        size = reflectors.shape[3]
        in_specs += [
            pl.BlockSpec((1, 1, count, size), lambda i, j, info: (0, half, block, 0)),
            pl.BlockSpec((1, 1, count, size), lambda i, j, info: (1, half, block, 0)),
            pl.BlockSpec((2 * size, tile), lambda i, j, info: (0, j)),
            pl.BlockSpec((2 * size, tile), lambda i, j, info: (0, j)),
            pl.BlockSpec((1, tile), lambda i, j, info: (0, j)),
            pl.BlockSpec((count, tile), lambda i, j, info: (block, j)),
        ]
        operands += [reflectors, reflectors, *s, scale, held]
        if out is not None:
            in_specs.append(pl.BlockSpec(memory_space=pl.ANY))
            operands.append(out)
            aliases = {len(operands): 0}
        out_shape = (2, held.shape[0], width)
        out_spec = pl.BlockSpec(
            (1, count, tile), lambda i, j, info: (half, block, jnp.where(i == pairs - 1, j, 0))
        )
    if pairs > 1:
        scratch.append(pltpu.VMEM((width // tile, count, tile), jnp.float32))
    return pl.pallas_call(
        functools.partial(rows_kernel, (pairs, parts, rows), last),
        grid_spec=pltpu.PrefetchScalarGridSpec(
            num_scalar_prefetch=1,
            grid=(pairs, width // tile),
            in_specs=in_specs,
            out_specs=out_spec,
            scratch_shapes=scratch,
        ),
        out_shape=jax.ShapeDtypeStruct(out_shape, jnp.float32),
        input_output_aliases=aliases,
    )(info, *operands)


def project_kernel(y_ref, q_ref, o_ref, q_high, q_low):
    @pl.when(pl.program_id(1) == 0)
    def _():
        q_high[...], q_low[...] = split2(q_ref[0])

    o_ref[0] = dot3(*split2(y_ref[0, 0].T), q_high[...], q_low[...])


def project(reflectors, q_halves):
    _, rows, depth = q_halves.shape
    size = reflectors.shape[3]
    return pl.pallas_call(
        project_kernel,
        grid=(2, 2),
        in_specs=[
            pl.BlockSpec((1, 1, rows, size), lambda h, i: (i, h, 0, 0)),
            pl.BlockSpec((1, rows, depth), lambda h, i: (h, 0, 0)),
        ],
        out_specs=pl.BlockSpec((1, size, depth), lambda h, i: (h, i, 0)),
        out_shape=jax.ShapeDtypeStruct((2, 2 * size, depth), jnp.float32),
        scratch_shapes=[pltpu.VMEM((rows, depth), jnp.bfloat16)] * 2,
        name="project",
    )(reflectors, q_halves)


def merge(
    q_halves, pole_values, weights, secular_roots, column_order, deflated, reflectors, triangles
):
    col_count, row_count = lax.axis_size("col"), lax.axis_size("row")
    me, my_row = lax.axis_index("col"), lax.axis_index("row")
    _, rows, depth = q_halves.shape
    width = 2 * depth
    exact = dict(precision=lax.Precision.HIGHEST)
    cut = rows // 2

    def swap(x, mask):
        return lax.ppermute(x, "col", [(i, i ^ mask) for i in range(col_count)])

    def row_swap(x, mask):
        return lax.ppermute(x, "row", [(i, i ^ mask) for i in range(row_count)])

    bits = [1 << b for b in range(1, (col_count - 1).bit_length())]
    near = [0] + bits
    far = [m for m in range(2, col_count, 2) if m not in bits]

    partner = swap(q_halves, 1)
    got = [{} for _ in range(2)]
    for h in range(2):
        own = [q_halves[h, :cut], q_halves[h, cut:]]
        for bit in bits:
            order = (1, 0) if bit == bits[0] else (0, 1)
            parts = {p: swap(own[p], bit) for p in order}
            got[h][bit] = [parts[0], parts[1]]
    for h in range(2):
        for m in far:
            set_bits = [b for b in bits if b & m]
            via = [set_bits[0], set_bits[-1]]
            got[h][m] = [swap(got[h][m ^ via[p]][p], via[p]) for p in range(2)]
        for m in bits + far:
            got[h][m + 1] = [swap(x, 1) for x in got[h][m]]

    r_part = project(reflectors, q_halves)
    share = r_part.shape[1] // row_count
    r_mine = lax.dynamic_slice_in_dim(r_part, my_row * share, share, axis=1)
    for m in range(1, row_count):
        away = lax.dynamic_slice_in_dim(r_part, (my_row ^ m) * share, share, axis=1)
        r_mine = r_mine + row_swap(away, m)
    r_all = lax.all_gather(r_mine, "col", axis=2, tiled=True)
    cross = lax.psum(jnp.einsum("hrb,hrd->bd", reflectors[0], reflectors[1], **exact), "row")

    zeds = weights * (1 - deflated).astype(jnp.float32)
    source = lax.dynamic_slice_in_dim(column_order, me * width, width)
    roots = jnp.take(jnp.where(deflated > 0, FAR, secular_roots), source)
    gone = roots > 1e38
    keys = jnp.where(gone, source, -1)
    c_high, c_low, total = make_cauchy(pole_values, zeds, roots, keys)
    scale = jnp.where(gone[None, :], 1.0, lax.rsqrt(total + EPSILON))

    def pieces_of(h, masks, parts):
        pieces = []
        for m in masks:
            if m == 0:
                pieces.append([[q_halves] * len(parts), [partner] * len(parts)])
            else:
                pieces.append([[got[h][m + k][p] for p in parts] for k in range(2)])
        return pieces

    held = []
    for h in range(2):
        held.append(rows_call(h, 0, near, pieces_of(h, near, (0, 1)), c_high, c_low))

    p_part = early_projection(r_all, c_high, c_low)
    p_stack = jnp.stack([p_part] + [row_swap(p_part, m) for m in range(1, row_count)])
    p_all = jnp.concatenate(
        [lax.dynamic_index_in_dim(p_stack, my_row ^ z, keepdims=False) for z in range(row_count)]
    )
    size = triangles.shape[1]
    upper = jnp.triu(triangles)
    s1 = jnp.dot(upper[1], p_all[size:], **exact)
    s0 = jnp.dot(upper[0], p_all[:size] - jnp.dot(cross, s1, **exact), **exact)
    s = -jnp.concatenate([s0, s1], axis=0)
    s_high = lax.reduce_precision(s, 8, 7)
    s = (s_high.astype(jnp.bfloat16), (s - s_high).astype(jnp.bfloat16))

    out = None
    for h in range(2):
        for block, parts in [(0, (0, 1))] if h == 0 else [(0, (0,)), (1, (1,))]:
            out = rows_call(
                h, block, far, pieces_of(h, far, parts), c_high, c_low,
                (reflectors, s, scale, held[h], out),
            )
    return out


def solution(mesh):
    placed = (P(None, "row", "col"), P(), P(), P(), P(), P(), P(None, None, "row", None), P())
    return jax.shard_map(
        merge, mesh=mesh, in_specs=placed, out_specs=P(None, "row", "col"), check_vma=False
    )
```

```python
import functools

import jax
import jax.numpy as jnp
from jax import lax
from jax.experimental import pallas as pl
from jax.experimental.pallas import tpu as pltpu
from jax.sharding import PartitionSpec as P


EPSILON = 1e-06
FAR = 3e38


def split2(x):
    high = x.astype(jnp.bfloat16)
    return high, (x - high.astype(jnp.float32)).astype(jnp.bfloat16)


def dot3(a_high, a_low, b_high, b_low):
    dot = functools.partial(jnp.dot, preferred_element_type=jnp.float32)
    return dot(a_high, b_high) + (dot(a_high, b_low) + dot(a_low, b_high))


def cauchy_kernel(pole_ref, zed_ref, root_ref, key_ref, high_ref, low_ref, total_ref, poles, zeds):
    step = pl.program_id(0)
    rows = high_ref.shape[0]
    chunk = 256

    @pl.when(step == 0)
    def _():
        total_ref[...] = jnp.zeros_like(total_ref)

    for ref, held in ((pole_ref, poles), (zed_ref, zeds)):
        held[...] = jnp.broadcast_to(ref[...], (8, rows)).T

    @pl.loop(0, rows // chunk)
    def _(i):
        at = pl.multiple_of(i * chunk, chunk)
        span = pl.ds(at, chunk)
        ratio = zeds[span, :1] / (poles[span, :1] - root_ref[...])
        total_ref[...] += jnp.sum(ratio * ratio, axis=0, keepdims=True)
        row_ids = step * rows + at + lax.broadcasted_iota(jnp.int32, ratio.shape, 0)
        value = jnp.where(row_ids == key_ref[...], 1.0, ratio)
        high_ref[span], low_ref[span] = split2(value)


def make_cauchy(poles, zeds, roots, keys):
    count, width = poles.shape[0], roots.shape[0]
    rows = count // 8
    vec = pl.BlockSpec((1, rows), lambda i: (0, i))
    line = pl.BlockSpec((1, width), lambda i: (0, 0))
    tile = pl.BlockSpec((rows, width), lambda i: (i, 0))
    part = jax.ShapeDtypeStruct((count, width), jnp.bfloat16)
    return pl.pallas_call(
        cauchy_kernel,
        grid=(count // rows,),
        in_specs=[vec, vec, line, line],
        out_specs=[tile, tile, line],
        out_shape=[part, part, jax.ShapeDtypeStruct((1, width), jnp.float32)],
        scratch_shapes=[pltpu.VMEM((rows, 8), jnp.float32)] * 2,
        name="cauchy",
    )(poles[None, :], zeds[None, :], roots[None, :], keys[None, :])


def early_kernel(count, info_ref, *refs):
    pieces, (ch_ref, cl_ref, o_ref, high, low) = refs[:count], refs[count:]
    depth = pieces[0].shape[2]
    odd = info_ref[0] > 0

    @pl.when(pl.program_id(0) == 0)
    def _():
        for i in range(count // 2):
            for h in range(2):
                mine, other = pieces[2 * i][h], pieces[2 * i + 1][h]
                ordered = (jnp.where(odd, other, mine), jnp.where(odd, mine, other))
                for core in range(2):
                    at = (i, h, slice(None), slice(core * depth, (core + 1) * depth))
                    high[at], low[at] = split2(ordered[core])

    total = 0.0
    for i in range(count // 2):
        for h in range(2):
            start = (h * (count // 2) + info_ref[1 + i]) * 2 * depth
            span = pl.ds(pl.multiple_of(start, 2 * depth), 2 * depth)
            total = total + dot3(high[i, h], low[i, h], ch_ref[span], cl_ref[span])
    o_ref[...] = total


def early_projection(me, pieces, c_high, c_low):
    _, rows, depth = pieces[0].shape
    count, width = c_high.shape
    tile = 256 if width % 256 == 0 else 128
    info = jnp.stack([me & 1] + [(me ^ m) >> 1 for m in range(0, len(pieces), 2)])
    col = pl.BlockSpec((count, tile), lambda j, info: (0, j))
    whole = pl.BlockSpec(pieces[0].shape, lambda j, info: (0, 0, 0))
    return pl.pallas_call(
        functools.partial(early_kernel, len(pieces)),
        grid_spec=pltpu.PrefetchScalarGridSpec(
            num_scalar_prefetch=1,
            grid=(width // tile,),
            in_specs=[whole] * len(pieces) + [col, col],
            out_specs=pl.BlockSpec((rows, tile), lambda j, info: (0, j)),
            scratch_shapes=[pltpu.VMEM((len(pieces) // 2, 2, rows, 2 * depth), jnp.bfloat16)] * 2,
        ),
        out_shape=jax.ShapeDtypeStruct((rows, width), jnp.float32),
        name="early",
    )(info.astype(jnp.int32), *pieces, c_high, c_low)


def rows_kernel(counts, last, begun, info_ref, *refs):
    refs = list(refs)
    pairs, parts, rows = counts
    sources = [[[refs.pop(0) for _ in range(parts)] for _ in range(2)] for _ in range(pairs)]
    high_ref, low_ref = refs.pop(0), refs.pop(0)
    if last:
        first_y, second_y, sh_ref, sl_ref, scale_ref, acc_ref = (refs.pop(0) for _ in range(6))
    elif begun:
        acc_ref = refs.pop(0)
    refs = refs[1:] if last == 2 else refs
    out_ref, staged, q_high, q_low, sems = refs[:5]
    depth = staged.shape[3]
    step, col = pl.program_id(0), pl.program_id(1)
    half, block, odd = info_ref[0], info_ref[1], info_ref[2]

    def copies(i):
        for core in range(2):
            slot = odd if core == 0 else 1 - odd
            for part in range(parts):
                ref = sources[i][core][part]
                if len(ref.shape) == 3:
                    ref = ref.at[half, pl.ds((block * parts + part) * rows, rows)]
                yield pltpu.make_async_copy(
                    ref, staged.at[slot, part], sems.at[core, part]
                )

    @pl.when(jnp.logical_and(step == 0, col == 0))
    def _():
        for copy in copies(0):
            copy.start()

    for i in range(pairs):

        @pl.when(jnp.logical_and(step == i, col == 0))
        def _():
            for copy in copies(i):
                copy.wait()

    @pl.when(col == 0)
    def _():
        for core in range(2):
            for part in range(parts):
                at = (slice(part * rows, (part + 1) * rows), slice(core * depth, (core + 1) * depth))
                q_high[at], q_low[at] = split2(staged[core, part])

    for i in range(pairs - 1):

        @pl.when(jnp.logical_and(step == i, col == 0))
        def _():
            for copy in copies(i + 1):
                copy.start()

    def emit(mixed):
        if last:
            out_ref[0] = (acc_ref[...] + mixed) * scale_ref[...]
        else:
            out_ref[...] = acc_ref[...] + mixed if begun else mixed

    if last:
        size = first_y.shape[3]

        @pl.when(jnp.logical_and(step == 0, col == 0))
        def _():
            for at, y_ref in ((2 * depth, first_y), (2 * depth + size, second_y)):
                span = slice(at, at + size)
                q_high[:, span], q_low[:, span] = split2(y_ref[0, 0])

    high, low = high_ref[...], low_ref[...]
    if last:
        keep = jnp.where(step == 0, 1.0, 0.0).astype(jnp.bfloat16) if pairs > 1 else None
        extra = [ref[...] if keep is None else ref[...] * keep for ref in (sh_ref, sl_ref)]
        high, low = jnp.concatenate([high, extra[0]]), jnp.concatenate([low, extra[1]])
    product = dot3(q_high[...], q_low[...], high, low)

    if pairs == 1:
        emit(product)
    else:
        total = refs[-1]

        @pl.when(step == 0)
        def _():
            total[col] = product

        if pairs > 2:

            @pl.when(jnp.logical_and(step > 0, step < pairs - 1))
            def _():
                total[col] += product

        @pl.when(step == pairs - 1)
        def _():
            emit(total[col] + product)


def rows_call(half, block, masks, pieces, c_high, c_low, finish=None, acc=None):
    me = lax.axis_index("col")
    chips = lax.axis_size("col") // 2
    pairs, parts = len(masks), len(pieces[0][0])
    rows, depth = pieces[-1][0][0].shape[-2:]
    width = c_high.shape[1]
    tile = 256 if width % 256 == 0 else 128
    head = [jnp.int32(half), jnp.int32(block), me & 1]
    info = jnp.stack(head + [half * chips + ((me ^ m) >> 1) for m in masks]).astype(jnp.int32)

    operands = [array for pair in pieces for piece in pair for array in piece]
    in_specs = [pl.BlockSpec(memory_space=pl.ANY)] * len(operands)
    cauchy = pl.BlockSpec((2 * depth, tile), lambda i, j, info: (info[3 + i], j))
    in_specs += [cauchy, cauchy]
    operands += [c_high, c_low]
    count = parts * rows
    scratch = [pltpu.VMEM((2, parts, rows, depth), jnp.float32)]
    inner = 2 * depth + (0 if finish is None else 2 * finish[0].shape[3])
    scratch += [pltpu.VMEM((count, inner), jnp.bfloat16)] * 2
    scratch += [pltpu.SemaphoreType.DMA((2, parts))]
    aliases, last = {}, 0
    if finish is None:
        out_shape = (count, width)
        out_spec = pl.BlockSpec((count, tile), lambda i, j, info: (0, jnp.where(i == pairs - 1, j, 0)))
        if acc is not None:
            in_specs.append(out_spec)
            operands.append(acc)
    else:
        reflectors, s, scale, held, out = finish
        last = 1 if out is None else 2
        size = reflectors.shape[3]
        in_specs += [
            pl.BlockSpec((1, 1, count, size), lambda i, j, info: (0, half, block, 0)),
            pl.BlockSpec((1, 1, count, size), lambda i, j, info: (1, half, block, 0)),
            pl.BlockSpec((2 * size, tile), lambda i, j, info: (0, j)),
            pl.BlockSpec((2 * size, tile), lambda i, j, info: (0, j)),
            pl.BlockSpec((1, tile), lambda i, j, info: (0, j)),
            pl.BlockSpec((count, tile), lambda i, j, info: (block, j)),
        ]
        operands += [reflectors, reflectors, *s, scale, held]
        if out is not None:
            in_specs.append(pl.BlockSpec(memory_space=pl.ANY))
            operands.append(out)
            aliases = {len(operands): 0}
        out_shape = (2, held.shape[0], width)
        out_spec = pl.BlockSpec(
            (1, count, tile), lambda i, j, info: (half, block, jnp.where(i == pairs - 1, j, 0))
        )
    if pairs > 1:
        scratch.append(pltpu.VMEM((width // tile, count, tile), jnp.float32))
    return pl.pallas_call(
        functools.partial(rows_kernel, (pairs, parts, rows), last, acc is not None),
        grid_spec=pltpu.PrefetchScalarGridSpec(
            num_scalar_prefetch=1,
            grid=(pairs, width // tile),
            in_specs=in_specs,
            out_specs=out_spec,
            scratch_shapes=scratch,
        ),
        out_shape=jax.ShapeDtypeStruct(out_shape, jnp.float32),
        input_output_aliases=aliases,
    )(info, *operands)


def project_kernel(y_ref, q_ref, o_ref, cross_ref, q_high, q_low, first_high, first_low):
    half, which = pl.program_id(0), pl.program_id(1)
    y = y_ref[0, 0]
    turned = split2(y.T)

    @pl.when(which == 0)
    def _():
        q_high[...], q_low[...] = split2(q_ref[0])
        first_high[...], first_low[...] = turned

    @pl.when(which == 1)
    def _():
        both = dot3(first_high[...], first_low[...], *split2(y))
        cross_ref[...] = jnp.where(half == 0, both, cross_ref[...] + both)

    o_ref[0] = dot3(*turned, q_high[...], q_low[...])


def project(reflectors, q_halves):
    _, rows, depth = q_halves.shape
    size = reflectors.shape[3]
    return pl.pallas_call(
        project_kernel,
        grid=(2, 2),
        in_specs=[
            pl.BlockSpec((1, 1, rows, size), lambda h, i: (i, h, 0, 0)),
            pl.BlockSpec((1, rows, depth), lambda h, i: (h, 0, 0)),
        ],
        out_specs=[
            pl.BlockSpec((1, size, depth), lambda h, i: (h, i, 0)),
            pl.BlockSpec((size, size), lambda h, i: (0, 0)),
        ],
        out_shape=[
            jax.ShapeDtypeStruct((2, 2 * size, depth), jnp.float32),
            jax.ShapeDtypeStruct((size, size), jnp.float32),
        ],
        scratch_shapes=[pltpu.VMEM((rows, depth), jnp.bfloat16)] * 2
        + [pltpu.VMEM((size, rows), jnp.bfloat16)] * 2,
        name="project",
    )(reflectors, q_halves)


def coefficient_kernel(at_ref, *refs):
    *pieces, triangles_ref, cross_ref, high_ref, low_ref, whole = refs
    share = pieces[0].shape[0]
    size = cross_ref.shape[0]
    for mask, piece in enumerate(pieces):
        start = pl.multiple_of((at_ref[0] ^ mask) * share, share)
        whole[pl.ds(start, share)] = piece[...]

    def times(a, b):
        return dot3(*split2(a), *split2(b))

    shape = (size, size)
    keep = lax.broadcasted_iota(jnp.int32, shape, 0) <= lax.broadcasted_iota(jnp.int32, shape, 1)
    upper = [jnp.where(keep, triangles_ref[i], 0.0) for i in range(2)]
    second = times(upper[1], whole[size:])
    first = times(upper[0], whole[:size] - times(cross_ref[...], second))
    high_ref[:size], low_ref[:size] = split2(-first)
    high_ref[size:], low_ref[size:] = split2(-second)


def coefficients(my_row, pieces, triangles, cross):
    size, width = cross.shape[0], pieces[0].shape[1]
    part = jax.ShapeDtypeStruct((2 * size, width), jnp.bfloat16)
    everything = pl.BlockSpec(memory_space=pltpu.VMEM)
    return pl.pallas_call(
        coefficient_kernel,
        in_specs=[pl.BlockSpec(memory_space=pltpu.SMEM)] + [everything] * (len(pieces) + 2),
        out_specs=[everything, everything],
        out_shape=[part, part],
        scratch_shapes=[pltpu.VMEM((2 * size, width), jnp.float32)],
        name="coefficients",
    )(my_row[None], *pieces, triangles, cross)


def merge(
    q_halves, pole_values, weights, secular_roots, column_order, deflated, reflectors, triangles
):
    col_count, row_count = lax.axis_size("col"), lax.axis_size("row")
    me, my_row = lax.axis_index("col"), lax.axis_index("row")
    _, rows, depth = q_halves.shape
    width = 2 * depth

    def swap(x, mask):
        return lax.ppermute(x, "col", [(i, i ^ mask) for i in range(col_count)])

    def row_swap(x, mask):
        return lax.ppermute(x, "row", [(i, i ^ mask) for i in range(row_count)])

    bits = [1 << b for b in range(1, (col_count - 1).bit_length())]
    near = [0] + bits
    far = [m for m in range(2, col_count, 2) if m not in bits]

    partner = swap(q_halves, 1)
    cut = rows // 2
    own = [[q_halves[0]], [q_halves[1, :cut], q_halves[1, cut:]]]

    def swap_all(parts, mask):
        return [swap(x, mask) for x in parts]

    got = [{bit: swap_all(own[h], bit) for bit in bits} for h in range(2)]
    for h in range(2):
        for m in far:
            set_bits = [b for b in bits if b & m]
            via = set_bits[0] if h == 0 else set_bits[-1]
            got[h][m] = swap_all(got[h][m ^ via], via)
        for m in bits + far:
            got[h][m + 1] = swap_all(got[h][m], 1)

    r_part, cross = project(reflectors, q_halves)
    share = r_part.shape[1] // row_count

    def for_row(row):
        return lax.dynamic_slice_in_dim(r_part, row * share, share, axis=1)

    near_r = for_row(my_row)
    for m in range(1, row_count):
        near_r = near_r + row_swap(for_row(my_row ^ m), m)
    cross = cross + sum(row_swap(cross, m) for m in range(1, row_count))
    r_pieces = {0: near_r}
    for m in range(2, col_count, 2):
        r_pieces[m] = swap(near_r, m)
    for m in range(0, col_count, 2):
        r_pieces[m + 1] = swap(r_pieces[m], 1)
    r_pieces = [r_pieces[m] for m in range(col_count)]

    zeds = weights * (1 - deflated).astype(jnp.float32)
    source = lax.dynamic_slice_in_dim(column_order, me * width, width)
    roots = jnp.take(jnp.where(deflated > 0, FAR, secular_roots), source)
    gone = roots > 1e38
    keys = jnp.where(gone, source, -1)
    c_high, c_low, total = make_cauchy(pole_values, zeds, roots, keys)
    scale = jnp.where(gone[None, :], 1.0, lax.rsqrt(total + EPSILON))

    def pieces_of(h, masks):
        return [
            [[q_halves] * (h + 1), [partner] * (h + 1)] if m == 0 else [got[h][m], got[h][m + 1]]
            for m in masks
        ]

    begun = rows_call(0, 0, near[:1], pieces_of(0, near[:1]), c_high, c_low)
    held = []
    for h, masks in enumerate((near[1:], near)):
        acc = None if h else begun
        pieces = pieces_of(h, masks)
        held.append(rows_call(h, 0, masks, pieces, c_high, c_low, acc=acc))

    p_part = early_projection(me, r_pieces, c_high, c_low)
    p_pieces = [p_part] + [row_swap(p_part, m) for m in range(1, row_count)]
    s = coefficients(my_row, p_pieces, triangles, cross)

    out = None
    for h in range(2):
        finish = (reflectors, s, scale, held[h], out)
        out = rows_call(h, 0, far, pieces_of(h, far), c_high, c_low, finish)
    return out


def solution(mesh):
    placed = (P(None, "row", "col"), P(), P(), P(), P(), P(), P(None, None, "row", None), P())
    return jax.shard_map(
        merge, mesh=mesh, in_specs=placed, out_specs=P(None, "row", "col"), check_vma=False
    )
```
